32 devices in a mesh: replica: 8 (over y, x, core), shard: 4 (over z).
Axes of the slice: x: 2, y: 2, z: 4, core: 2. Of those that a mesh axis runs over, the one named last changes fastest.
Arguments:
- layer_input: bfloat16 [64, 512, 768], P(('replica', 'shard')), may hold values from -6 to 6
- out_grad: bfloat16 [64, 512, 768], P(('replica', 'shard')), may hold values from -6 to 6
- seq_lengths: int32 [64], replicated, may hold values from 64 to 512, as said below
- deal_order: int32 [64], replicated, may hold values from 0 to 63, as said below
- w_query: bfloat16 [768, 768], P('shard'), may hold values from -0.21875 to 0.21875
- b_query: bfloat16 [768], P('shard'), may hold values from -1.75 to 1.75
- w_key: bfloat16 [768, 768], P('shard'), may hold values from -0.21875 to 0.21875
- w_value: bfloat16 [768, 768], P('shard'), may hold values from -0.21875 to 0.21875
- b_value: bfloat16 [768], P('shard'), may hold values from -0.0625 to 0.0625
- w_output: bfloat16 [768, 768], P('shard'), may hold values from -4 to 4
- b_output: bfloat16 [768], P('shard'), may hold values from -1.25 to 1.25
- first_gain: bfloat16 [768], P('shard'), may hold values from 0.099609375 to 1.8984375
- first_shift: bfloat16 [768], P('shard'), may hold values from -1.75 to 1.75
- w_inner: bfloat16 [768, 3072], P('shard'), may hold values from -0.21875 to 0.21875
- b_inner: bfloat16 [3072], P('shard'), may hold values from -1.75 to 1.75
- w_outer: bfloat16 [3072, 768], P('shard'), may hold values from -0.109375 to 0.109375
- b_outer: bfloat16 [768], P('shard'), may hold values from -1.75 to 1.75
- second_gain: bfloat16 [768], P('shard'), may hold values from 0.099609375 to 1.8984375
- second_shift: bfloat16 [768], P('shard'), may hold values from -1.75 to 1.75
Outputs:
- layer_output: bfloat16 [64, 512, 768], P(('replica', 'shard'))
- input_grad: bfloat16 [64, 512, 768], P(('replica', 'shard'))
- grad_wquery: float32 [768, 768], P('shard')
- grad_bquery: float32 [768], P('shard')
- grad_wkey: float32 [768, 768], P('shard')
- grad_wvalue: float32 [768, 768], P('shard')
- grad_bvalue: float32 [768], P('shard')
- grad_woutput: float32 [768, 768], P('shard')
- grad_boutput: float32 [768], P('shard')
- grad_firstgain: float32 [768], P('shard')
- grad_firstshift: float32 [768], P('shard')
- grad_winner: float32 [768, 3072], P('shard')
- grad_binner: float32 [3072], P('shard')
- grad_wouter: float32 [3072, 768], P('shard')
- grad_bouter: float32 [768], P('shard')
- grad_secondgain: float32 [768], P('shard')
- grad_secondshift: float32 [768], P('shard')
The draws below stay inside these ranges and needn't reach their ends.
Inputs may be any that keep to these rules, and one draw needn't show every extreme that they name: `seq_lengths`: every length is at least 64; the two sequences placed in slots 2 j and 2 j + 1 have lengths that sum to at most 576; some sequence has exactly 512. A permutation of the 64 sequences: slot i receives sequence deal_order[i] of the given order.
All inputs are finite; a program needn't handle non-finite values.
Results may differ from the reference program's by a relative error of at most 0.02.
Values may be sent and summed in bfloat16 or wider, within the bound.
No kernel may reach another device: no remote copies, remote signals or barrier semaphores. Data moves between devices by JAX's collectives and lax.ppermute only.
A program may use at most 128 MiB of HBM per device.

```python
import math
import jax
import jax.numpy as jnp
from jax import lax

D = 768
HEADS = 12
FF = 3072
MAXLEN = 512
MINLEN = 64
NSEQ = 64


def pair_table(key):
    base_key = jax.random.fold_in(key, 17)
    key_lead = jax.random.fold_in(base_key, 1)
    key_trail = jax.random.fold_in(base_key, 2)
    key_pick = jax.random.fold_in(base_key, 3)
    key_place = jax.random.fold_in(base_key, 4)
    pair_count = NSEQ // 2
    lead_len = jax.random.randint(key_lead, (pair_count,), MINLEN, MAXLEN + 1)
    chosen = jax.random.randint(key_pick, (), 0, pair_count)
    lead_len = jnp.where(jnp.arange(pair_count) == chosen, MAXLEN, lead_len)
    trail_len = jax.random.randint(key_trail, (pair_count,), MINLEN, MAXLEN + MINLEN - lead_len + 1)
    slot_len = jnp.stack([lead_len, trail_len], axis=1).reshape(NSEQ).astype(jnp.int32)
    placing = jax.random.permutation(key_place, NSEQ).astype(jnp.int32)
    return (slot_len, placing)


def draw_deal_order(key, part):
    slot_len, placing = pair_table(key)
    return placing


def draw_seq_lengths(key, part):
    slot_len, placing = pair_table(key)
    return jnp.zeros((NSEQ,), jnp.int32).at[placing].set(slot_len)


def levels(own_key, shape, pieces, least, high):
    def one(axis_at, parts):
        draws = jax.random.uniform(jax.random.fold_in(jax.random.fold_in(own_key, 6), axis_at), (parts,), jnp.float32, least / len(pieces), high / len(pieces))
        return jnp.repeat(jnp.exp(draws), shape[axis_at] // parts).reshape((-1,) + (1,) * (len(shape) - axis_at - 1))

    gain = one(*pieces[0])
    for cut in pieces[1:]:
        gain = gain * one(*cut)
    return gain


def scatter_about(rng, shape, scale, limit, pieces=(), held_as=jnp.bfloat16):
    values = jax.random.normal(rng, shape, jnp.float32) * scale
    if len(pieces) > 0:
        values = levels(rng, shape, pieces, -0.22, 0.18) * values
    return jnp.clip(values, min=-limit, max=limit).astype(held_as)


def setup_inputs(seed: int = 0) -> dict:
    splits = jax.random.split(jax.random.key(seed), 20)
    return {
        "layer_input": scatter_about(splits[0], (NSEQ, MAXLEN, D), 1.0, 6.0, ((0, 32),)),
        "out_grad": scatter_about(splits[1], (NSEQ, MAXLEN, D), 1.0, 6.0, ((0, 32),)),
        "seq_lengths": draw_seq_lengths(jax.random.fold_in(splits[19], 71), 0),
        "deal_order": draw_deal_order(jax.random.fold_in(splits[19], 71), 0),
        "w_query": scatter_about(splits[4], (D, D), D ** -0.5, 0.21875, ((0, 4),)),
        "b_query": scatter_about(splits[5], (D,), 0.3, 1.75, ((0, 4),)),
        "w_key": scatter_about(splits[6], (D, D), D ** -0.5, 0.21875, ((0, 4),)),
        "w_value": scatter_about(splits[7], (D, D), D ** -0.5, 0.21875, ((0, 4),)),
        "b_value": scatter_about(splits[8], (D,), 0.01, 0.0625, ((0, 4),)),
        "w_output": scatter_about(splits[9], (D, D), 2 ** -0.5, 4.0, ((0, 4),)),
        "b_output": scatter_about(splits[10], (D,), 0.2, 1.25, ((0, 4),)),
        "first_gain": jnp.clip(1.0 + 0.18 * jax.random.normal(splits[11], (D,), jnp.float32), 0.099609375, 1.8984375).astype(jnp.bfloat16),
        "first_shift": scatter_about(splits[12], (D,), 0.3, 1.75, ((0, 4),)),
        "w_inner": scatter_about(splits[13], (D, FF), D ** -0.5, 0.21875, ((0, 4),)),
        "b_inner": scatter_about(splits[14], (FF,), 0.3, 1.75, ((0, 4),)),
        "w_outer": scatter_about(splits[15], (FF, D), FF ** -0.5, 0.109375, ((0, 4),)),
        "b_outer": scatter_about(splits[16], (D,), 0.3, 1.75, ((0, 4),)),
        "second_gain": jnp.clip(1.0 + 0.18 * jax.random.normal(splits[17], (D,), jnp.float32), 0.099609375, 1.8984375).astype(jnp.bfloat16),
        "second_shift": scatter_about(splits[18], (D,), 0.3, 1.75, ((0, 4),)),
    }


NORM_EPS = 1e-12
SCORE_SCALE = 0.125
MASK_VALUE = -1e+30

@jax.custom_vjp
def low(v):
    return lax.optimization_barrier(v.astype(jnp.bfloat16)).astype(jnp.float32)

@jax.custom_vjp
def low_back(v):
    return v

def low_keep(v):
    return (low(v), None)

def low_pass(kept, grad):
    return (grad,)

def back_keep(v):
    return (v, None)

def back_low(kept, grad):
    return (low(grad),)
low.defvjp(low_keep, low_pass)
low_back.defvjp(back_keep, back_low)

def normalize(values, gain_vec, shift_vec):
    center = values - lax.optimization_barrier(jnp.mean(values, axis=-1, keepdims=True))
    inverse = lax.rsqrt(lax.optimization_barrier(jnp.mean(center * center, axis=-1, keepdims=True)) + NORM_EPS)
    return center * inverse * gain_vec + shift_vec

def gelu_exact(values):
    return 0.5 * values * (1.0 + lax.erf(values * (1.0 / math.sqrt(2.0))))

def pack_pair(leading, trailing, lead_len, trail_len, capacity):
    seq_rows = leading.shape[0]
    features = leading.shape[1]
    row_ids = jnp.arange(seq_rows, dtype=jnp.int32)[:, None]
    leading = jnp.where(row_ids < lead_len, leading, jnp.zeros_like(leading))
    trailing = jnp.where(row_ids < trail_len, trailing, jnp.zeros_like(trailing))
    head_part = jnp.concatenate([leading, jnp.zeros((capacity - seq_rows, features), leading.dtype)], axis=0)
    padded = jnp.concatenate([jnp.zeros((capacity, features), leading.dtype), trailing, jnp.zeros((capacity - seq_rows, features), leading.dtype)], axis=0)
    tail_part = lax.dynamic_slice_in_dim(padded, (capacity - lead_len).astype(jnp.int32), capacity, 0)
    return head_part + tail_part

def unpack_pair(packed, lead_len, trail_len, seq_rows):
    features = packed.shape[1]
    row_ids = jnp.arange(seq_rows, dtype=jnp.int32)[:, None]
    leading = jnp.where(row_ids < lead_len, packed[:seq_rows], jnp.zeros((seq_rows, features), packed.dtype))
    extended = jnp.concatenate([packed, jnp.zeros((seq_rows, features), packed.dtype)], axis=0)
    trailing = lax.dynamic_slice_in_dim(extended, lead_len.astype(jnp.int32), seq_rows, 0)
    trailing = jnp.where(row_ids < trail_len, trailing, jnp.zeros_like(trailing))
    return jnp.stack([leading, trailing], axis=0)

def forward(params, packed_rows, key_valid):
    w_query, b_query, w_key, w_value, b_value, w_output, b_output, first_gain, first_shift, w_inner, b_inner, w_outer, b_outer, second_gain, second_shift = params
    highest = lax.Precision.HIGHEST
    row_count = packed_rows.shape[0]
    query_rows = low_back(low(jnp.dot(packed_rows, w_query, precision=highest, preferred_element_type=jnp.float32) + b_query))
    key_rows = low_back(low(jnp.dot(packed_rows, w_key, precision=highest, preferred_element_type=jnp.float32)))
    value_rows = low_back(low(jnp.dot(packed_rows, w_value, precision=highest, preferred_element_type=jnp.float32) + b_value))
    query_heads = query_rows.reshape(row_count, HEADS, -1)
    key_heads = key_rows.reshape(row_count, HEADS, -1)
    value_heads = value_rows.reshape(row_count, HEADS, -1)
    scores = low_back(jnp.einsum('qhd,khd->hqk', query_heads, key_heads, precision=highest) * SCORE_SCALE)
    scores = jnp.where(key_valid[None, None, :], scores, MASK_VALUE)
    row_max = lax.optimization_barrier(jnp.max(scores, axis=-1, keepdims=True))
    exp_scores = jnp.exp(scores - row_max)
    attn_probs = low(exp_scores / lax.optimization_barrier(jnp.sum(exp_scores, axis=-1, keepdims=True)))
    mix_rows = jnp.einsum('hqk,khd->qhd', attn_probs, value_heads, precision=highest).reshape(row_count, -1)
    mix_rows = low_back(low(mix_rows))
    branch = low_back(jnp.dot(mix_rows, w_output, precision=highest, preferred_element_type=jnp.float32) + b_output)
    first_out = normalize(packed_rows + branch, first_gain, first_shift)
    inner_pre = low_back(jnp.dot(low(first_out), w_inner, precision=highest, preferred_element_type=jnp.float32) + b_inner)
    act_rows = low(gelu_exact(inner_pre))
    outer_out = low_back(jnp.dot(act_rows, w_outer, precision=highest, preferred_element_type=jnp.float32) + b_outer)
    return normalize(first_out + outer_out, second_gain, second_shift)

def reference(layer_input, out_grad, seq_lengths, deal_order, w_query, b_query, w_key, w_value, b_value, w_output, b_output, first_gain, first_shift, w_inner, b_inner, w_outer, b_outer, second_gain, second_shift):
    params = tuple((param.astype(jnp.float32) for param in (w_query, b_query, w_key, w_value, b_value, w_output, b_output, first_gain, first_shift, w_inner, b_inner, w_outer, b_outer, second_gain, second_shift)))
    capacity = MAXLEN + MINLEN
    pair_count = deal_order.shape[0] // 2

    def one_row(totals, index):
        lead_seq = deal_order[2 * index]
        trail_seq = deal_order[2 * index + 1]
        lead_len = seq_lengths[lead_seq]
        trail_len = seq_lengths[trail_seq]
        packed_in = pack_pair(layer_input[lead_seq], layer_input[trail_seq], lead_len, trail_len, capacity).astype(jnp.float32)
        packed_cot = pack_pair(out_grad[lead_seq], out_grad[trail_seq], lead_len, trail_len, capacity).astype(jnp.float32)
        key_valid = jnp.arange(capacity, dtype=jnp.int32) < lead_len + trail_len
        out_rows, pull_back = jax.vjp(lambda prm, rows_in: forward(prm, rows_in, key_valid), params, packed_in)
        grad_params, grad_rows = pull_back(packed_cot)
        totals = jax.tree.map(lambda left_val, right_val: left_val + right_val, totals, grad_params)
        out_slots = unpack_pair(out_rows, lead_len, trail_len, MAXLEN).astype(jnp.bfloat16)
        grad_slots = unpack_pair(grad_rows, lead_len, trail_len, MAXLEN).astype(jnp.bfloat16)
        return (totals, (out_slots, grad_slots))
    zero_grads = tuple((jnp.zeros(param.shape, jnp.float32) for param in params))
    totals, (out_slots, grad_slots) = lax.scan(one_row, zero_grads, jnp.arange(pair_count, dtype=jnp.int32))
    out_slots = out_slots.reshape(2 * pair_count, MAXLEN, -1)
    grad_slots = grad_slots.reshape(2 * pair_count, MAXLEN, -1)
    inverse_order = jnp.argsort(deal_order).astype(jnp.int32)
    layer_output = jnp.take(out_slots, inverse_order, axis=0)
    input_grad = jnp.take(grad_slots, inverse_order, axis=0)
    return (layer_output, input_grad, totals[0], totals[1], totals[2], totals[3], totals[4], totals[5], totals[6], totals[7], totals[8], totals[9], totals[10], totals[11], totals[12], totals[13], totals[14])
```

```python
import functools
import math

import jax
import jax.numpy as jnp
from jax import lax
from jax.experimental import pallas as pl
from jax.experimental.pallas import tpu as pltpu
from jax.sharding import PartitionSpec as P

HEADS = 12
MAXLEN = 512
MINLEN = 64
TILE = 16
NORM_EPS = 1e-12
SCORE_SCALE = 0.125
LOG2E = 1.4426950408889634
EXP_SCALE = SCORE_SCALE * LOG2E
MASK_VALUE = -1e30
BOTH = ("replica", "shard")
BF = jnp.bfloat16
F32 = jnp.float32
I32 = jnp.int32

SMEM = functools.partial(pl.BlockSpec, memory_space=pltpu.SMEM)
VMEM = functools.partial(pl.BlockSpec, memory_space=pltpu.VMEM)
BIG = pltpu.CompilerParams(vmem_limit_bytes=60 * 1024 * 1024)


def dot_rows(left_op, right_op):
    return jnp.dot(left_op, right_op, preferred_element_type=F32)


def dot_left(left_op, right_op):
    return lax.dot_general(left_op, right_op, (((0,), (0,)), ((), ())), preferred_element_type=F32)


def dot_right(left_op, right_op):
    return lax.dot_general(left_op, right_op, (((1,), (1,)), ((), ())), preferred_element_type=F32)


def normalize(values, gain_vec, shift_vec):
    center = values - jnp.mean(values, axis=-1, keepdims=True)
    inverse = lax.rsqrt(jnp.mean(center * center, axis=-1, keepdims=True) + NORM_EPS)
    normed = center * inverse
    return (normed * gain_vec + shift_vec, normed, inverse)


def normalize_back(upstream, normed, inverse, gain_vec):
    scaled = upstream * gain_vec
    centered = (
        scaled
        - jnp.mean(scaled, axis=-1, keepdims=True)
        - normed * jnp.mean(scaled * normed, axis=-1, keepdims=True)
    )
    return (inverse * centered, jnp.sum(upstream * normed, axis=0), jnp.sum(upstream, axis=0))


def gelu_exact(values):
    return 0.5 * values * (1.0 + lax.erf(values * (1.0 / math.sqrt(2.0))))


def gelu_slope(values):
    cumulative = 0.5 * (1.0 + lax.erf(values * (1.0 / math.sqrt(2.0))))
    density = jnp.exp(-0.5 * values * values) * (1.0 / math.sqrt(2.0 * math.pi))
    return cumulative + values * density


def route_kernel(order, lens, me, src_of, dst_of, info, slot_of, keep, len_keep, len_move):
    count = order.shape[0]
    devices = count // 2

    def place(i, carry):
        slot_of[order[i]] = i
        return carry

    def clear(d, carry):
        keep[d] = -1
        return carry

    lax.fori_loop(0, count, place, 0)
    lax.fori_loop(0, devices, clear, 0)

    def start(d, carry):
        def unassigned(seq):
            return keep[lax.shift_right_logical(seq, 1)] < 0

        def step(seq):
            host = lax.shift_right_logical(seq, 1)
            mate = order[lax.bitwise_xor(slot_of[seq], 1)]
            home = lax.shift_right_logical(mate, 1)
            keep[host] = lax.bitwise_and(seq, 1)
            src_of[host] = home
            dst_of[home] = host
            len_keep[host] = lens[seq]
            len_move[host] = lens[mate]
            return lax.bitwise_xor(mate, 1)

        lax.while_loop(unassigned, step, 2 * d)
        return carry

    lax.fori_loop(0, devices, start, 0)
    mine = me[0]
    info[0] = keep[mine]
    info[1] = len_keep[mine]
    info[2] = len_move[mine]
    info[3] = ((len_keep[mine] + (TILE - 1)) // TILE) * TILE


def route(deal_order, seq_lengths, device_pos):
    count = deal_order.shape[0]
    devices = count // 2
    return pl.pallas_call(
        route_kernel,
        out_shape=(
            jax.ShapeDtypeStruct((devices,), I32),
            jax.ShapeDtypeStruct((devices,), I32),
            jax.ShapeDtypeStruct((4,), I32),
        ),
        in_specs=[SMEM(), SMEM(), SMEM()],
        out_specs=(SMEM(), SMEM(), SMEM()),
        scratch_shapes=[
            pltpu.SMEM((count,), I32),
            pltpu.SMEM((devices,), I32),
            pltpu.SMEM((devices,), I32),
            pltpu.SMEM((devices,), I32),
        ],
        name="route",
    )(deal_order, seq_lengths, device_pos.reshape(1))


def pack_kernel(info, kept, moved, out):
    blocks = out.shape[0] // TILE
    seq_blocks = moved.shape[0] // TILE
    shift = info[3] // TILE
    row = lax.broadcasted_iota(I32, (TILE, 1), 0)

    def one(b, carry):
        kb = jnp.minimum(b, seq_blocks - 1)
        mb = jnp.clip(b - shift, 0, seq_blocks - 1)
        here = pl.ds(pl.multiple_of(b * TILE, TILE), TILE)
        a = kept[0, pl.ds(pl.multiple_of(kb * TILE, TILE), TILE), :]
        m = moved[pl.ds(pl.multiple_of(mb * TILE, TILE), TILE), :]
        in_a = b * TILE + row < info[1]
        at = b * TILE - info[3] + row
        in_m = (at >= 0) & (at < info[2])
        out[here, :] = jnp.where(in_a, a, jnp.where(in_m, m, jnp.zeros_like(m)))
        return carry

    lax.fori_loop(0, blocks, one, 0, unroll=False)


def pack(info, given, moved, capacity):
    _, seq_rows, features = given.shape
    return pl.pallas_call(
        pack_kernel,
        out_shape=jax.ShapeDtypeStruct((capacity, features), given.dtype),
        grid_spec=pltpu.PrefetchScalarGridSpec(
            num_scalar_prefetch=1,
            grid=(1,),
            in_specs=[
                pl.BlockSpec((1, seq_rows, features), lambda i, t: (t[0], 0, 0)),
                pl.BlockSpec((seq_rows, features), lambda i, t: (0, 0)),
            ],
            out_specs=pl.BlockSpec((capacity, features), lambda i, t: (0, 0)),
        ),
        name="pack",
    )(info, given, moved)


def unpack_kernel(info, packed, final, moved):
    blocks = packed.shape[0] // TILE
    seq_blocks = moved.shape[0] // TILE
    shift = info[3] // TILE
    row = lax.broadcasted_iota(I32, (TILE, 1), 0)

    def one(b, carry):
        here = pl.ds(pl.multiple_of(b * TILE, TILE), TILE)
        a = packed[here, :]
        mb = jnp.minimum(b + shift, blocks - 1)
        m = packed[pl.ds(pl.multiple_of(mb * TILE, TILE), TILE), :]
        at = b * TILE + row
        final[0, here, :] = jnp.where(at < info[1], a, jnp.zeros_like(a))
        moved[here, :] = jnp.where(at < info[2], m, jnp.zeros_like(m))
        return carry

    lax.fori_loop(0, seq_blocks, one, 0, unroll=False)


def unpack(info, packed, seq_rows):
    capacity, features = packed.shape
    return pl.pallas_call(
        unpack_kernel,
        out_shape=(
            jax.ShapeDtypeStruct((2, seq_rows, features), packed.dtype),
            jax.ShapeDtypeStruct((seq_rows, features), packed.dtype),
        ),
        grid_spec=pltpu.PrefetchScalarGridSpec(
            num_scalar_prefetch=1,
            grid=(1,),
            in_specs=[pl.BlockSpec((capacity, features), lambda i, t: (0, 0))],
            out_specs=(
                pl.BlockSpec((1, seq_rows, features), lambda i, t: (t[0], 0, 0)),
                pl.BlockSpec((seq_rows, features), lambda i, t: (0, 0)),
            ),
        ),
        name="unpack",
    )(info, packed)


def spread_rows(rows, table):
    devices = table.shape[0]
    seq_rows, features = rows.shape
    pieces = rows.reshape(devices, seq_rows // devices, features)
    held = lax.all_to_all(pieces, BOTH, split_axis=0, concat_axis=0, tiled=True)
    held = jnp.take(held, table, axis=0)
    out = lax.all_to_all(held, BOTH, split_axis=0, concat_axis=0, tiled=True)
    return out.reshape(seq_rows, features)


def flip(axis_size, bit):
    return [(i, i ^ bit) for i in range(axis_size)]


def shift_by(axis_size, step):
    return [(i, (i + step) % axis_size) for i in range(axis_size)]


def row_bits(replicas, shard_rows):
    bits = []
    bit = 2
    while bit < replicas and (shard_rows // 2 ** (len(bits) + 1)) % TILE == 0 and len(bits) < 2:
        bits.append(bit)
        bit *= 2
    return tuple(bits)


def row_block(replica, order):
    block = 0
    for bit in order:
        block = 2 * block + lax.bitwise_and(replica // bit, 1)
    return block


def share(held, replicas, order):
    for bit in order:
        held = jnp.concatenate([held, lax.ppermute(held, "replica", flip(replicas, bit))], axis=0)
    return held, lax.ppermute(held, "replica", flip(replicas, 1))


def gather_pieces(piece, replicas, shards, order):
    parts = [piece]
    for step in range(1, shards):
        parts.append(lax.ppermute(piece, "shard", shift_by(shards, step)))
    return share(jnp.stack(parts), replicas, order)


def my_piece(weight, replica, order):
    rows, cols = weight.shape
    take = rows // 2 ** len(order)
    return lax.dynamic_slice(
        weight,
        (row_block(replica, order) * take, lax.bitwise_and(replica, 1) * (cols // 2)),
        (take, cols // 2),
    )


def place_of(block, core_flip, pos, order, shards):
    replica = lax.bitwise_xor(pos[0], core_flip)
    rest = block // shards
    for i, bit in enumerate(order):
        replica = lax.bitwise_xor(replica, lax.bitwise_and(rest // 2**i, 1) * bit)
    shard = lax.rem(pos[1] - lax.rem(block, shards) + shards, shards)
    return replica, shard


def attn_weights_kernel(order, shards, pos, held, recv, w_qkv, w_out, vectors):
    take = (held.shape[1] - TILE) // 4
    half = held.shape[2]
    split = 2 ** len(order)
    groups = half // 128

    for flipped, source in ((0, held), (1, recv)):

        def one(b, carry):
            replica, shard = place_of(b, flipped, pos, order, shards)
            row = pl.multiple_of((shard * split + row_block(replica, order)) * take, TILE)
            core = lax.bitwise_and(replica, 1)
            for w in range(3):
                for g in range(groups):
                    col = pl.multiple_of(core * (half * 3) + g * 384 + w * 128, 128)
                    w_qkv[pl.ds(row, take), pl.ds(col, 128)] = source[
                        b, w * take : (w + 1) * take, g * 128 : (g + 1) * 128
                    ]
            w_out[pl.ds(row, take), pl.ds(pl.multiple_of(core * half, 128), half)] = source[
                b, 3 * take : 4 * take, :
            ]
            return carry

        lax.fori_loop(0, source.shape[0], one, 0)
    for b in range(shards):
        _, shard = place_of(b, 0, pos, order, shards)
        vectors[shard] = held[b, 4 * take :, :]


def attn_weights(pos, held, recv, order, shards, features):
    half = held.shape[2]
    return pl.pallas_call(
        functools.partial(attn_weights_kernel, order, shards),
        out_shape=(
            jax.ShapeDtypeStruct((features, 3 * features), BF),
            jax.ShapeDtypeStruct((features, features), BF),
            jax.ShapeDtypeStruct((shards, TILE, half), BF),
        ),
        in_specs=[SMEM(), VMEM(), VMEM()],
        out_specs=(VMEM(), VMEM(), VMEM()),
        compiler_params=BIG,
        name="attn_weights",
    )(pos, held, recv)


def one_weight_kernel(order, shards, pos, held, recv, out):
    take, half = held.shape[1:]
    split = 2 ** len(order)

    for flipped, source in ((0, held), (1, recv)):

        def one(b, carry):
            replica, shard = place_of(b, flipped, pos, order, shards)
            row = pl.multiple_of((shard * split + row_block(replica, order)) * take, TILE)
            col = pl.multiple_of(lax.bitwise_and(replica, 1) * half, 128)
            out[pl.ds(row, take), pl.ds(col, half)] = source[b]
            return carry

        lax.fori_loop(0, source.shape[0], one, 0)


def one_weight(pos, held, recv, order, shards):
    blocks, take, half = held.shape
    return pl.pallas_call(
        functools.partial(one_weight_kernel, order, shards),
        out_shape=jax.ShapeDtypeStruct((blocks * take, 2 * half), BF),
        in_specs=[SMEM(), VMEM(), VMEM()],
        out_specs=VMEM(),
        compiler_params=BIG,
        name="one_weight",
    )(pos, held, recv)


def row_parts(rows, size):
    return [(at, min(size, rows - at)) for at in range(0, rows, size)]


def split_three(values):
    high = values.astype(BF)
    rest = values - high.astype(F32)
    mid = rest.astype(BF)
    return high, mid, (rest - mid.astype(F32)).astype(BF)


def attend_kernel(info, qkv, out, lse, stats):
    rows = qkv.shape[0]
    lane = lax.broadcasted_iota(I32, (1, 128), 1)
    key_row = lax.broadcasted_iota(I32, (1, rows), 1)
    at = key_row - info[3]
    valid = (key_row < info[1]) | ((at >= 0) & (at < info[2]))
    bias = jnp.where(valid, 0.0, MASK_VALUE).astype(F32)
    keys = qkv[:, 128:256]
    values = qkv[:, 256:384]
    for start, size in row_parts(rows, 128):
        query = qkv[start : start + size, 0:128]
        mixes, totals = [], []
        for h in range(2):
            mine = (lane >= 64) if h else (lane < 64)
            scores = dot_right(jnp.where(mine, query, jnp.zeros_like(query)), keys)
            scores = scores * EXP_SCALE + bias
            top = jnp.max(scores, axis=1, keepdims=True)
            weights = jnp.exp2(scores - top)
            total = jnp.sum(weights, axis=1, keepdims=True)
            mixes.append(dot_rows(weights.astype(BF), values) * (1.0 / total))
            totals.append(top + jnp.log2(total))
        out[start : start + size, :] = jnp.where(lane < 64, mixes[0], mixes[1]).astype(BF)
        stats[start : start + size, :] = jnp.where(lane < 64, totals[0], totals[1])
    pick_row = lax.broadcasted_iota(I32, (TILE, 128), 0)
    pick_lane = lax.broadcasted_iota(I32, (TILE, 128), 1)
    pick = jnp.where(pick_lane == pick_row * 64, 1.0, 0.0).astype(BF)
    across = sum(dot_right(pick, part) for part in split_three(stats[...]))
    lse[...] = across[:8]


def attend(info, qkv):
    rows, width = qkv.shape
    pairs = width // 384
    return pl.pallas_call(
        attend_kernel,
        out_shape=(
            jax.ShapeDtypeStruct((rows, pairs * 128), BF),
            jax.ShapeDtypeStruct((pairs * 8, rows), F32),
        ),
        grid_spec=pltpu.PrefetchScalarGridSpec(
            num_scalar_prefetch=1,
            grid=(pairs,),
            in_specs=[pl.BlockSpec((rows, 384), lambda g, t: (0, g))],
            out_specs=(
                pl.BlockSpec((rows, 128), lambda g, t: (0, g)),
                pl.BlockSpec((8, rows), lambda g, t: (g, 0)),
            ),
            scratch_shapes=[pltpu.VMEM((rows, 128), F32)],
        ),
        cost_estimate=pl.CostEstimate(
            flops=4 * rows * rows * 128 * pairs * 2,
            bytes_accessed=2 * rows * width,
            transcendentals=rows * rows * pairs * 2,
        ),
        name="attend",
    )(info, qkv)


def attend_back_kernel(info, qkv, grad, mix, lse, dqkv, sums, dq):
    rows = qkv.shape[0]
    lane = lax.broadcasted_iota(I32, (1, 128), 1)
    query = qkv[:, 0:128]
    grads = grad[...]
    pick_row = lax.broadcasted_iota(I32, (TILE, 128), 0)
    pick_lane = lax.broadcasted_iota(I32, (TILE, 128), 1)
    pick = jnp.where(lax.shift_right_logical(pick_lane, 6) == pick_row, 1.0, 0.0).astype(BF)
    product = grads.astype(F32) * mix[...].astype(F32)
    row_dots = sum(dot_right(pick, part) for part in split_three(product))
    halves = []
    for h in range(2):
        mine = (lane >= 64) if h else (lane < 64)
        halves.append(
            (
                mine,
                jnp.where(mine, query, jnp.zeros_like(query)),
                jnp.where(mine, grads, jnp.zeros_like(grads)),
                lse[h : h + 1, :],
                row_dots[h : h + 1, :],
            )
        )
    sum_k = jnp.zeros((1, 128), F32)
    sum_v = jnp.zeros((1, 128), F32)
    for index, (start, size) in enumerate(row_parts(rows, 128)):
        keys = qkv[start : start + size, 128:256]
        values = qkv[start : start + size, 256:384]
        row = lax.broadcasted_iota(I32, (size, 1), 0) + start
        at = row - info[3]
        valid = (row < info[1]) | ((at >= 0) & (at < info[2]))
        dk = jnp.zeros((size, 128), F32)
        dv = jnp.zeros((size, 128), F32)
        for h, (mine, query_h, grads_h, lse_h, dots_h) in enumerate(halves):
            keys_h = jnp.where(mine, keys, jnp.zeros_like(keys))
            scores = dot_right(keys, query_h) * EXP_SCALE
            probs = jnp.where(valid, jnp.exp2(scores - lse_h), 0.0)
            dv = dv + dot_rows(probs.astype(BF), grads_h)
            prob_grad = dot_right(values, grads_h)
            score_grad = (probs * (prob_grad - dots_h)).astype(BF)
            dk = dk + dot_rows(score_grad, query_h)
            part = dot_left(score_grad, keys_h)
            if index == 0 and h == 0:
                dq[...] = part
            else:
                dq[...] += part
        dk_low = (dk * SCORE_SCALE).astype(BF)
        dv_low = dv.astype(BF)
        dqkv[start : start + size, 128:256] = dk_low
        dqkv[start : start + size, 256:384] = dv_low
        sum_v = sum_v + jnp.sum(dv_low.astype(F32), axis=0, keepdims=True)
    dq_low = (dq[...] * SCORE_SCALE).astype(BF)
    dqkv[:, 0:128] = dq_low
    sums[...] = jnp.zeros_like(sums)
    sums[0:1, 0:128] = jnp.sum(dq_low.astype(F32), axis=0, keepdims=True)
    sums[0:1, 256:384] = sum_v


def attend_back(info, qkv, grad, mix, lse):
    rows, width = qkv.shape
    pairs = width // 384
    return pl.pallas_call(
        attend_back_kernel,
        out_shape=(
            jax.ShapeDtypeStruct((rows, width), BF),
            jax.ShapeDtypeStruct((pairs * 8, 384), F32),
        ),
        grid_spec=pltpu.PrefetchScalarGridSpec(
            num_scalar_prefetch=1,
            grid=(pairs,),
            in_specs=[
                pl.BlockSpec((rows, 384), lambda g, t: (0, g)),
                pl.BlockSpec((rows, 128), lambda g, t: (0, g)),
                pl.BlockSpec((rows, 128), lambda g, t: (0, g)),
                pl.BlockSpec((8, rows), lambda g, t: (g, 0)),
            ],
            out_specs=(
                pl.BlockSpec((rows, 384), lambda g, t: (0, g)),
                pl.BlockSpec((8, 384), lambda g, t: (g, 0)),
            ),
            scratch_shapes=[pltpu.VMEM((rows, 128), F32)],
        ),
        cost_estimate=pl.CostEstimate(
            flops=10 * rows * rows * 128 * pairs * 2,
            bytes_accessed=6 * rows * width,
            transcendentals=rows * rows * pairs * 2,
        ),
        name="attend_back",
    )(info, qkv, grad, mix, lse)


def core_cols(array, core):
    half = array.shape[1] // 2
    return lax.dynamic_slice_in_dim(array, core * half, half, 1)


def core_sum(left_op, right_op, core, replicas):
    send = dot_left(left_op, core_cols(right_op, 1 - core)).astype(BF)
    got = lax.ppermute(send, "replica", flip(replicas, 1))
    return (dot_left(left_op, core_cols(right_op, core)) + got.astype(F32)).astype(BF)


def reduce_rest(part, replica, shard, replicas, shards, order):
    rows, cols = part.shape
    part = part.reshape(shards, rows // shards, cols)
    for bit in order:
        mine = lax.bitwise_and(replica // bit, 1)
        view = part.reshape(shards, 2, part.shape[1] // 2, cols)
        send = lax.dynamic_index_in_dim(view, 1 - mine, 1, keepdims=False)
        keep = lax.dynamic_index_in_dim(view, mine, 1, keepdims=False)
        got = lax.ppermute(send, "replica", flip(replicas, bit))
        part = (keep.astype(F32) + got.astype(F32)).astype(BF)
    bit = 2
    while bit < replicas:
        if bit not in order:
            got = lax.ppermute(part, "replica", flip(replicas, bit))
            part = (part.astype(F32) + got.astype(F32)).astype(BF)
        bit *= 2
    total = lax.dynamic_index_in_dim(part, shard, 0, keepdims=False).astype(F32)
    for step in range(1, shards):
        send = lax.dynamic_index_in_dim(part, lax.rem(shard + step, shards), 0, keepdims=False)
        total = total + lax.ppermute(send, "shard", shift_by(shards, step)).astype(F32)
    return share(total.astype(BF)[None], replicas, tuple(reversed(order)))


def place_grads_kernel(order, parts, pos, held, recv, *outs):
    take = held.shape[1]
    exchange = tuple(reversed(order))
    for flipped, source in ((0, held), (1, recv)):
        for b in range(source.shape[0]):
            replica, _ = place_of(b, flipped, pos, exchange, 1)
            core = lax.bitwise_and(replica, 1)
            row = pl.multiple_of(row_block(replica, order) * take, TILE)
            for out, pieces in zip(outs, parts):
                half = out.shape[1] // 2
                for to, at, width in pieces:
                    col = pl.multiple_of(core * half + to, 128)
                    out[pl.ds(row, take), pl.ds(col, width)] = source[b, :, at : at + width].astype(F32)


def place_grads(pos, held, recv, order, shapes, parts):
    return pl.pallas_call(
        functools.partial(place_grads_kernel, order, parts),
        out_shape=tuple(jax.ShapeDtypeStruct(shape, F32) for shape in shapes),
        in_specs=[SMEM(), VMEM(), VMEM()],
        out_specs=tuple(VMEM() for _ in shapes),
        compiler_params=BIG,
        name="place_grads",
    )(pos, held, recv)


def sum_all(values, devices):
    bit = 1
    while bit < devices:
        values = values + lax.ppermute(values, BOTH, flip(devices, bit))
        bit *= 2
    return values


def on_device(
    layer_input,
    out_grad,
    seq_lengths,
    deal_order,
    w_query,
    b_query,
    w_key,
    w_value,
    b_value,
    w_output,
    b_output,
    first_gain,
    first_shift,
    w_inner,
    b_inner,
    w_outer,
    b_outer,
    second_gain,
    second_shift,
):
    replicas = lax.axis_size("replica")
    shards = lax.axis_size("shard")
    devices = replicas * shards
    replica = lax.axis_index("replica")
    shard = lax.axis_index("shard")
    core = lax.bitwise_and(replica, 1)
    pos = jnp.stack([replica, shard]).astype(I32)
    seq_rows = layer_input.shape[1]
    features = layer_input.shape[2]
    hidden = w_inner.shape[1]
    capacity = MAXLEN + MINLEN + TILE
    src_of, dst_of, info = route(deal_order, seq_lengths, replica * shards + shard)
    other = 1 - info[0]

    moved_in = spread_rows(lax.dynamic_index_in_dim(layer_input, other, 0, keepdims=False), src_of)
    packed_in = pack(info, layer_input, moved_in, capacity)
    cot_rows = lax.dynamic_index_in_dim(out_grad, other, 0, keepdims=False)
    cot_rows, _ = lax.optimization_barrier((cot_rows, moved_in))
    packed_cot = pack(info, out_grad, spread_rows(cot_rows, src_of), capacity)

    bits = row_bits(replicas, w_query.shape[0])
    order_a, order_b = bits, tuple(reversed(bits))
    shard_vec = jnp.concatenate(
        [
            b_query,
            b_value,
            b_output,
            first_gain,
            first_shift,
            b_outer,
            second_gain,
            second_shift,
            b_inner,
        ]
    )
    half = features // 2
    vec_rows = shard_vec.reshape(-1, half) if shard_vec.shape[0] % half == 0 else None
    if vec_rows is None:
        lacking = -shard_vec.shape[0] % half
        vec_rows = jnp.pad(shard_vec, (0, lacking)).reshape(-1, half)
    vec_rows = jnp.pad(vec_rows, ((0, TILE - vec_rows.shape[0]), (0, 0)))
    attn_piece = jnp.concatenate(
        [my_piece(w, replica, order_a) for w in (w_query, w_key, w_value, w_output)] + [vec_rows],
        axis=0,
    )
    held, recv = gather_pieces(attn_piece, replicas, shards, order_a)
    wqkv_full, wo_full, vectors = attn_weights(pos, held, recv, order_a, shards, features)
    inner_piece = my_piece(w_inner, replica, order_b)
    wi_full = one_weight(pos, *gather_pieces(inner_piece, replicas, shards, order_b), order_b, shards)
    outer_piece = my_piece(w_outer, replica, order_a)
    wout_full = one_weight(pos, *gather_pieces(outer_piece, replicas, shards, order_a), order_a, shards)
    flat = vectors.reshape(shards, -1)
    per = features // shards
    named = [flat[:, i * per : (i + 1) * per].reshape(features).astype(F32) for i in range(8)]
    bq, bv, bo, gain_one, shift_one, bout, gain_two, shift_two = named
    bi = flat[:, 8 * per : 8 * per + hidden // shards].reshape(hidden).astype(F32)
    pairs = features // 128
    bqkv = jnp.stack(
        [bq.reshape(pairs, 128), jnp.zeros((pairs, 128), F32), bv.reshape(pairs, 128)], axis=1
    ).reshape(3 * features)

    qkv = (dot_rows(packed_in, wqkv_full) + bqkv).astype(BF)
    mix_low, lse = attend(info, qkv)
    branch = dot_rows(mix_low, wo_full) + bo
    first_out, normed_one, inverse_one = normalize(
        packed_in.astype(F32) + branch, gain_one, shift_one
    )
    hidden_low = first_out.astype(BF)
    inner_pre = dot_rows(hidden_low, wi_full) + bi
    act_low = gelu_exact(inner_pre).astype(BF)
    outer_out = dot_rows(act_low, wout_full) + bout
    packed_out, normed_two, inverse_two = normalize(first_out + outer_out, gain_two, shift_two)
    final_out, out_moved = unpack(info, packed_out.astype(BF), seq_rows)
    out_back = spread_rows(out_moved, dst_of)
    final_out = lax.dynamic_update_slice(final_out, out_back[None], (other, 0, 0))

    second_back, grad_secondgain, grad_secondshift = normalize_back(
        packed_cot.astype(F32), normed_two, inverse_two, gain_two
    )
    outer_grad = second_back.astype(BF)
    grad_bouter = jnp.sum(outer_grad.astype(F32), axis=0)
    inner_grad = (dot_right(outer_grad, wout_full) * gelu_slope(inner_pre)).astype(BF)
    grad_binner = jnp.sum(inner_grad.astype(F32), axis=0)
    part_outer = core_sum(act_low, outer_grad, core, replicas)
    part_inner = core_sum(hidden_low, inner_grad, core, replicas)
    first_total = second_back + dot_right(inner_grad, wi_full)
    first_back, grad_firstgain, grad_firstshift = normalize_back(
        first_total, normed_one, inverse_one, gain_one
    )
    branch_grad = first_back.astype(BF)
    grad_boutput = jnp.sum(branch_grad.astype(F32), axis=0)
    part_output = core_sum(mix_low, branch_grad, core, replicas)
    mix_grad = dot_right(branch_grad, wo_full).astype(BF)
    dqkv, dqkv_sums = attend_back(info, qkv, mix_grad, mix_low, lse)
    input_packed = first_back + dot_right(dqkv, wqkv_full)
    final_back, back_moved = unpack(info, input_packed.astype(BF), seq_rows)
    back_rows = spread_rows(back_moved, dst_of)
    final_back = lax.dynamic_update_slice(final_back, back_rows[None], (other, 0, 0))
    part_qkv = core_sum(packed_in, dqkv, core, replicas)

    inner_half = hidden // 2
    shard_rows = features // shards
    (grad_wouter,) = place_grads(
        pos,
        *reduce_rest(part_outer, replica, shard, replicas, shards, order_a),
        order_a,
        [(hidden // shards, features)],
        [[(0, 0, half)]],
    )
    grad_winner, grad_woutput = place_grads(
        pos,
        *reduce_rest(
            jnp.concatenate([part_inner, part_output], axis=1),
            replica,
            shard,
            replicas,
            shards,
            order_b,
        ),
        order_b,
        [(shard_rows, hidden), (shard_rows, features)],
        [[(0, 0, inner_half)], [(0, inner_half, half)]],
    )
    grad_wquery, grad_wkey, grad_wvalue = place_grads(
        pos,
        *reduce_rest(part_qkv, replica, shard, replicas, shards, order_a),
        order_a,
        [(shard_rows, features)] * 3,
        [[(g * 128, g * 384 + w * 128, 128) for g in range(half // 128)] for w in range(3)],
    )
    sums = dqkv_sums.reshape(pairs, 8, 3, 128)[:, 0]
    grad_bquery = sums[:, 0].reshape(features)
    grad_bvalue = sums[:, 2].reshape(features)
    totals = sum_all(
        jnp.concatenate(
            [
                v.reshape(-1, 128)
                for v in (
                    grad_bquery,
                    grad_bvalue,
                    grad_boutput,
                    grad_firstgain,
                    grad_firstshift,
                    grad_bouter,
                    grad_secondgain,
                    grad_secondshift,
                    grad_binner,
                )
            ],
            axis=0,
        ),
        devices,
    ).reshape(-1)
    vec = [
        lax.dynamic_slice_in_dim(totals, i * features + shard * per, per, 0) for i in range(8)
    ]
    grad_binner = lax.dynamic_slice_in_dim(
        totals, 8 * features + shard * (hidden // shards), hidden // shards, 0
    )
    return (
        final_out,
        final_back,
        grad_wquery,
        vec[0],
        grad_wkey,
        grad_wvalue,
        vec[1],
        grad_woutput,
        vec[2],
        vec[3],
        vec[4],
        grad_winner,
        grad_binner,
        grad_wouter,
        vec[5],
        vec[6],
        vec[7],
    )


def solution(mesh):
    rows = P(BOTH, None, None)
    matrix = P("shard", None)
    vector = P("shard")
    in_specs = (
        rows,
        rows,
        P(),
        P(),
        matrix,
        vector,
        matrix,
        matrix,
        vector,
        matrix,
        vector,
        vector,
        vector,
        matrix,
        vector,
        matrix,
        vector,
        vector,
        vector,
    )
    out_specs = (
        rows,
        rows,
        matrix,
        vector,
        matrix,
        matrix,
        vector,
        matrix,
        vector,
        vector,
        vector,
        matrix,
        vector,
        matrix,
        vector,
        vector,
        vector,
    )
    return jax.shard_map(
        on_device, mesh=mesh, in_specs=in_specs, out_specs=out_specs, check_vma=False
    )
```
